32 devices in a mesh: group: 2 (over y), expert: 4 (over z), head: 4 (over x, core).
Axes of the slice: x: 2, y: 2, z: 4, core: 2. Of those that a mesh axis runs over, the one named last changes fastest.
Arguments:
- residual_in: bfloat16 [1024, 2048], P(('group', 'expert'), 'head'), parts along dimension 0, may hold values from -5.1 to 5.1
- norm_gain: bfloat16 [2048], P('head'), may hold values from 0.29882812 to 3
- expert_ids: int32 [1024, 8], P(('group', 'expert')), parts along dimension 0, may hold values from 0 to 63, as said below
- route_scores: float32 [1024, 8], P(('group', 'expert')), parts along dimension 0, may hold values from -0.4 to 2.2
- gate_weight: bfloat16 [64, 2048, 1024], P('expert', None, 'head'), may hold values from -0.125 to 0.125
- up_weight: bfloat16 [64, 2048, 1024], P('expert', None, 'head'), may hold values from -0.125 to 0.125
- down_weight: bfloat16 [64, 1024, 2048], P('expert', 'head'), may hold values from -0.1875 to 0.1875
- gate_exp: int32 [64, 16, 8], P('expert', None, 'head'), may hold values from -2 to 1
- up_exp: int32 [64, 16, 8], P('expert', None, 'head'), may hold values from -2 to 1
- down_exp: int32 [64, 8, 16], P('expert', 'head'), may hold values from -2 to 1
Outputs:
- mixed: bfloat16 [1024, 2048], P(('group', 'expert'), 'head'), parts along dimension 0
The draws below stay inside these ranges and needn't reach their ends.
There are 2 independent parts, one for each index of `group`. The reference program is written for one: setup_inputs(seed, part) draws one part's arguments, and reference() takes and returns one part's arrays. A program takes and returns all parts, laid end to end along the dimension named above; an argument that names none is the same for every part. Nothing has to cross between parts.
Inputs may be any that keep to these rules, and one draw needn't show every extreme that they name: `expert_ids`: each row names 8 different experts. In the rows of one aligned block of 128 tokens no expert is named more than 24 times, and in every block at least one expert (up to five) is named exactly 24 times.
All inputs are finite; a program needn't handle non-finite values.
Results may differ from the reference program's by a relative error of at most 0.014.
Values may be sent and summed in bfloat16 or wider, within the bound.
No kernel may reach another device: no remote copies, remote signals or barrier semaphores. Data moves between devices by JAX's collectives and lax.ppermute only.
A program may use at most 192 MiB of HBM per device.

```python
import math
import jax
import jax.numpy as jnp
from jax import lax

D = 2048
FF = 1024
EXPERTS = 64
TOP = 8
QB = 128
TOK_DEV = 128
CAP = 24
TOKENS = 512
N_HEAD = 4


def draw_residual_in(key, part):
    key_noise = jax.random.fold_in(key, 0)
    column = jnp.arange(D, dtype=jnp.float32) / (D - 1)
    col_scale = jnp.power(10.0, column - 0.5) * 0.3
    values = jax.random.truncated_normal(key_noise, -4.0, 4.0, (TOKENS, D), jnp.float32) * col_scale[None, :]
    return values.astype(jnp.bfloat16)


def route_plan(key):
    key_hot, key_blocks = jax.random.split(key)
    hot_expert = jax.random.randint(key_hot, (), 0, EXPERTS).astype(jnp.int32)
    cycle_size = EXPERTS - 5

    def one_block(block_key):
        key_order, key_member, key_offset, key_rotate = jax.random.split(block_key, 4)
        order = ((hot_expert + 1 + jax.random.permutation(key_order, EXPERTS - 1).astype(jnp.int32)) % EXPERTS).astype(jnp.int32)
        hot_table = jnp.concatenate((hot_expert[None], order[:4]))
        cycle_table = order[4:]
        position = jax.random.permutation(key_member, TOK_DEV).astype(jnp.int32)
        is_hot = position < 5 * CAP
        hot_pick = hot_table[jnp.minimum(position // CAP, 4)]
        offset = (jax.random.permutation(key_offset, TOK_DEV).astype(jnp.int32) % cycle_size).astype(jnp.int32)
        slot_range = jnp.arange(TOP, dtype=jnp.int32)
        window = cycle_table[(offset[:, None] + slot_range[None, :]) % cycle_size]
        with_hot = jnp.concatenate((hot_pick[:, None], window[:, :TOP - 1]), axis=1)
        chosen = jnp.where(is_hot[:, None], with_hot, window)
        rotation = jax.random.randint(key_rotate, (TOK_DEV, 1), 0, TOP).astype(jnp.int32)
        order_index = (slot_range[None, :] + rotation) % TOP
        picked = jnp.take_along_axis(chosen, order_index, axis=1)
        leading = order_index == 0
        return (picked, leading)
    block_keys = jax.random.split(key_blocks, TOKENS // TOK_DEV)
    picked, leading = jax.vmap(one_block)(block_keys)
    return (picked.reshape(TOKENS, TOP).astype(jnp.int32), leading.reshape(TOKENS, TOP))


def draw_expert_ids(key, part):
    return route_plan(key)[0]


def draw_route_scores(key, part):
    leading = route_plan(key)[1]
    key_low, key_high = jax.random.split(jax.random.fold_in(key, 11))
    lower = jax.random.uniform(key_low, (TOKENS, TOP), jnp.float32, -0.3, 0.3)
    upper = jax.random.uniform(key_high, (TOKENS, TOP), jnp.float32, 1.0, 2.0)
    return jnp.where(leading, upper, lower).astype(jnp.float32)


def with_ends(values, own_key, least, largest):
    index_at = [jax.random.randint(jax.random.fold_in(own_key, axis), (), 0, length) for axis, length in enumerate(values.shape)]
    main_axis = values.shape.index(max(values.shape))
    next_to = index_at[:main_axis] + [(index_at[main_axis] + 1) % values.shape[main_axis]] + index_at[main_axis + 1:]
    return values.at[tuple(index_at)].set(least).at[tuple(next_to)].set(largest)


def level_of(key, dims, shards, low, largest):
    def one(dim, parts):
        draws = jax.random.uniform(jax.random.fold_in(jax.random.fold_in(key, 6), dim), (parts,), jnp.float32, low / len(shards), largest / len(shards))
        return jnp.repeat(jnp.exp(draws), dims[dim] // parts).reshape((-1,) + (1,) * (len(dims) - dim - 1))

    gain = one(*shards[0])
    for cut in shards[1:]:
        gain = gain * one(*cut)
    return gain


def scatter_about(key, dims, scale, most, cuts=(), kind=jnp.bfloat16):
    result = jax.random.normal(key, dims, jnp.float32) * scale
    if len(cuts) > 0:
        result = level_of(key, dims, cuts, -0.22, 0.18) * result
    return jnp.clip(result, min=-most, max=most).astype(kind)


def setup_inputs(seed: int = 0, part: int = 0) -> dict:
    seeds = jax.random.split(jax.random.key(seed), 11)
    part_keys = jax.random.split(jax.random.fold_in(seeds[10], part), 11)
    residual_in = draw_residual_in(jax.random.fold_in(jax.random.fold_in(seeds[10], part), 71), part)
    norm_gain = jnp.clip(jnp.exp(math.log(3.0) - 2.306499 * jax.random.uniform(seeds[1], (D,), jnp.float32) ** level_of(seeds[1], (D,), ((0, 4),), -0.2, 0.2)), 0.29882812, 3.0).astype(jnp.bfloat16)
    expert_ids = draw_expert_ids(jax.random.fold_in(jax.random.fold_in(seeds[10], part), 71), part)
    route_scores = draw_route_scores(jax.random.fold_in(jax.random.fold_in(seeds[10], part), 71), part)
    gate_weight = scatter_about(seeds[4], (EXPERTS, D, FF), D ** -0.5, 0.125, ((0, 4), (2, 4)))
    up_weight = scatter_about(seeds[5], (EXPERTS, D, FF), D ** -0.5, 0.125, ((0, 4), (2, 4)))
    down_weight = scatter_about(seeds[6], (EXPERTS, FF, D), FF ** -0.5, 0.1875, ((0, 4), (1, 4)))
    gate_exp = with_ends(jax.random.randint(seeds[7], (EXPERTS, D // QB, FF // QB), -2, 2), jax.random.fold_in(seeds[7], 1), -2, 1).astype(jnp.int32)
    up_exp = with_ends(jax.random.randint(seeds[8], (EXPERTS, D // QB, FF // QB), -2, 2), jax.random.fold_in(seeds[8], 1), -2, 1).astype(jnp.int32)
    down_exp = with_ends(jax.random.randint(seeds[9], (EXPERTS, FF // QB, D // QB), -2, 2), jax.random.fold_in(seeds[9], 1), -2, 1).astype(jnp.int32)
    return dict(residual_in=residual_in, norm_gain=norm_gain, expert_ids=expert_ids, route_scores=route_scores, gate_weight=gate_weight, up_weight=up_weight, down_weight=down_weight, gate_exp=gate_exp, up_exp=up_exp, down_exp=down_exp)


EPSILON = 1e-06

def power_two(exponent):
    magnitude = jnp.left_shift(jnp.ones_like(exponent), jnp.abs(exponent)).astype(jnp.float32)
    return jnp.where(exponent >= 0, magnitude, 1.0 / magnitude)

def dequantize(weight, exponent, block_size):
    experts_here, row_count, col_count = weight.shape
    factor = power_two(exponent).astype(jnp.bfloat16)
    shaped = weight.reshape(experts_here, row_count // block_size, block_size, col_count // block_size, block_size)
    return (shaped * factor[:, :, None, :, None]).reshape(experts_here, row_count, col_count)

def reference(residual_in, norm_gain, expert_ids, route_scores, gate_weight, up_weight, down_weight, gate_exp, up_exp, down_exp):
    values = residual_in.astype(jnp.float32)
    square = lax.optimization_barrier(jnp.mean(values * values, axis=1, keepdims=True))
    normed = (values * lax.rsqrt(square + EPSILON) * norm_gain.astype(jnp.float32)).astype(jnp.bfloat16)
    raised = jnp.exp(route_scores)
    weights = (raised / lax.optimization_barrier(jnp.sum(raised, axis=1, keepdims=True))).astype(jnp.bfloat16)
    blocks = TOKENS // TOK_DEV
    buffer_rows = blocks * CAP
    grouped = expert_ids.reshape(blocks, TOK_DEV * TOP)
    onehot = (grouped[:, :, None] == jnp.arange(EXPERTS, dtype=jnp.int32)[None, None, :]).astype(jnp.int32)
    earlier = jnp.cumsum(onehot, axis=1) - onehot
    within = lax.optimization_barrier(jnp.sum(earlier * onehot, axis=2))
    block_base = jnp.arange(blocks, dtype=jnp.int32)[:, None] * CAP
    slot_index = (grouped * buffer_rows + block_base + within).reshape(TOKENS, TOP).astype(jnp.int32)
    token_numbers = jnp.repeat(jnp.arange(TOKENS, dtype=jnp.int32), TOP) + 1
    token_of = jnp.zeros((EXPERTS * buffer_rows,), jnp.int32).at[slot_index.reshape(-1)].set(token_numbers)
    filled = token_of > 0
    source = jnp.maximum(token_of - 1, 0)
    gathered = jnp.where(filled[:, None], normed[source], jnp.zeros((), jnp.bfloat16))
    expert_rows = gathered.reshape(EXPERTS, buffer_rows, D)
    hidden_slice = FF // N_HEAD

    def one_expert(operands):
        rows_here, gate_w, up_w, down_w, gate_e, up_e, down_e = operands
        gate_full = dequantize(gate_w[None], gate_e[None], QB)[0]
        up_full = dequantize(up_w[None], up_e[None], QB)[0]
        down_full = dequantize(down_w[None], down_e[None], QB)[0]
        gate_out = jnp.dot(rows_here, gate_full, preferred_element_type=jnp.float32)
        up_out = jnp.dot(rows_here, up_full, preferred_element_type=jnp.float32)
        activation = (jax.nn.silu(gate_out) * up_out).astype(jnp.bfloat16)
        running = jnp.zeros((buffer_rows, D), jnp.float32)
        for head_part in range(N_HEAD):
            lower_bound = head_part * hidden_slice
            partial_value = jnp.dot(activation[:, lower_bound:lower_bound + hidden_slice], down_full[lower_bound:lower_bound + hidden_slice], preferred_element_type=jnp.float32)
            running = running + lax.optimization_barrier(partial_value.astype(jnp.bfloat16)).astype(jnp.float32)
        return running
    outputs = lax.map(one_expert, (expert_rows, gate_weight, up_weight, down_weight, gate_exp, up_exp, down_exp))
    outputs = outputs.reshape(EXPERTS * buffer_rows, D)
    combined = jnp.zeros((TOKENS, D), jnp.float32)
    for route_index in range(TOP):
        combined = combined + weights[:, route_index:route_index + 1].astype(jnp.float32) * outputs[slot_index[:, route_index]]
    return (values + combined).astype(jnp.bfloat16)
```

```python
import functools

import jax
import jax.numpy as jnp
from jax import lax
from jax.experimental import pallas as pl
from jax.experimental.pallas import tpu as pltpu
from jax.sharding import PartitionSpec as P

QB = 128
CAP = 24
EXTRA = 16
EPSILON = 1e-06
MIB = 1 << 20


def power_two(exponent):
    magnitude = jnp.left_shift(jnp.ones_like(exponent), jnp.abs(exponent)).astype(jnp.float32)
    return jnp.where(exponent >= 0, magnitude, 1.0 / magnitude)


def pack_kernel(rows_ref, gain_ref, ids_ref, scores_ref, out_ref):
    tokens, width = rows_ref.shape
    top = ids_ref.shape[0]
    out_ref[:tokens, :] = rows_ref[...]
    raised = jnp.exp(scores_ref[...])
    weights = raised / jnp.sum(raised, axis=0, keepdims=True)
    routes = jnp.concatenate((ids_ref[...].astype(jnp.float32), weights), axis=1)
    if width > 2 * tokens:
        routes = jnp.concatenate((routes, jnp.zeros((top, width - 2 * tokens), jnp.float32)), axis=1)
    gain = jnp.broadcast_to(gain_ref[...].astype(jnp.float32), (EXTRA - top, width))
    out_ref[tokens:, :] = jnp.concatenate((routes, gain), axis=0).astype(jnp.bfloat16)


def scaled(block, factor):
    parts = []
    for i, value in enumerate(factor):
        piece = block[i * QB : (i + 1) * QB]
        by = jnp.full((16, QB), value, jnp.float32).astype(jnp.bfloat16)
        parts.append((piece.reshape(QB // 16, 16, QB) * by[None]).reshape(QB, QB))
    return parts[0] if len(parts) == 1 else jnp.concatenate(parts, axis=0)


def up_kernel(n_head, n_block, split, place_ref, gate_fac, up_fac, *refs):
    n_piece = n_head * n_block if split else 1
    pieces = refs[:n_piece]
    gate_ref, up_ref, act_ref, comb_ref, normed, taken, slots = refs[n_piece:]

    def piece(f, j):
        return pieces[f * n_block + j] if split else pieces[0].at[f, j]

    experts, features, hidden = gate_ref.shape
    width = features // n_head
    tokens = normed.shape[0] // n_block
    pair = 2 * tokens
    slot = 2 * CAP
    cols = hidden // QB
    top = 8
    for j in range(n_block):
        total = jnp.zeros((tokens, 1), jnp.float32)
        for f in range(n_head):
            value = piece(f, j)[:tokens, :].astype(jnp.float32)
            total = total + jnp.sum(value * value, axis=1, keepdims=True)
        scale = lax.rsqrt(total / features + EPSILON)
        for f in range(n_head):
            value = piece(f, j)[:tokens, :].astype(jnp.float32)
            gain = piece(f, j)[tokens + top : tokens + top + 8, :].astype(jnp.float32)[0:1, :]
            normed[pl.ds(j * tokens, tokens), pl.ds(f * width, width)] = (
                value * scale * gain
            ).astype(jnp.bfloat16)
    first = place_ref[n_head]
    row = lax.broadcasted_iota(jnp.int32, (pair, pair), 0)
    col = lax.broadcasted_iota(jnp.int32, (pair, pair), 1)
    before = ((row < col) & ((row >= tokens) | (col < tokens))).astype(jnp.bfloat16)
    expert = (lax.broadcasted_iota(jnp.int32, (experts, pair), 0) + first).astype(jnp.float32)
    second = lax.broadcasted_iota(jnp.int32, (experts, pair), 1) >= tokens
    slot_no = lax.broadcasted_iota(jnp.int32, (slot, pair), 0).astype(jnp.float32)
    for p in range(n_block // 2):
        lists = [piece(0, 2 * p + i)[tokens : tokens + top, : 2 * tokens].astype(jnp.float32) for i in range(2)]
        ids = jnp.concatenate([x[:, :tokens] for x in lists], axis=1)
        weights = jnp.concatenate([x[:, tokens:] for x in lists], axis=1)
        named = jnp.zeros((experts, pair), jnp.float32)
        weight = jnp.zeros((experts, pair), jnp.float32)
        for k in range(top):
            same = ids[k : k + 1, :] == expert
            named = jnp.where(same, 1.0, named)
            weight = jnp.where(same, weights[k : k + 1, :], weight)
        rank = jnp.dot(named.astype(jnp.bfloat16), before, preferred_element_type=jnp.float32)
        target = jnp.where(named > 0, rank + jnp.where(second, float(CAP), 0.0), -1.0)
        back = []
        for e in range(experts):
            here = target[e : e + 1, :] == slot_no
            taken[pl.ds(e * slot, slot), :] = jnp.where(here, 1.0, 0.0).astype(jnp.bfloat16)
            back.append(jnp.where(here, weight[e : e + 1, :], 0.0))
        comb_ref[p] = jnp.transpose(jnp.concatenate(back, axis=0)).astype(jnp.bfloat16)
        step = min(features, 256)
        for n in range(features // step):
            rows = jnp.dot(
                taken[...],
                normed[pl.ds(p * pair, pair), pl.ds(n * step, step)],
                preferred_element_type=jnp.float32,
            ).astype(jnp.bfloat16)
            slots[:, pl.ds(p * slot, slot), pl.ds(n * step, step)] = rows.reshape(experts, slot, step)

    per_piece = width // QB

    def one_expert(e, carry):
        outs = []
        for ref, fac in ((gate_ref, gate_fac), (up_ref, up_fac)):
            acc = None
            for f in range(n_head):
                start = pl.multiple_of(place_ref[f] * width, width)
                left = slots[e, :, pl.ds(f * width, width)]
                base = (e * (features // QB) + place_ref[f] * per_piece) * cols
                block = ref[e, pl.ds(start, width), :]
                right = [
                    scaled(
                        block[:, n * QB : (n + 1) * QB],
                        [fac[base + i * cols + n] for i in range(per_piece)],
                    )
                    for n in range(cols)
                ]
                right = right[0] if cols == 1 else jnp.concatenate(right, axis=1)
                term = jnp.dot(left, right, preferred_element_type=jnp.float32)
                acc = term if acc is None else acc + term
            outs.append(acc)
        gate_out, up_out = outs
        act = gate_out / (1.0 + jnp.exp(-gate_out)) * up_out
        act_ref[e] = act.astype(jnp.bfloat16)
        return carry

    lax.fori_loop(0, experts, one_expert, 0)


def down_kernel(chunks, n_head, place_ref, down_fac, act_ref, comb_ref, down_ref, *refs):
    outs, (partial,) = refs[: len(chunks)], refs[len(chunks) :]
    experts, hidden, features = down_ref.shape
    width = features // n_head
    n_pair, pair, _ = comb_ref.shape
    slot = 2 * CAP
    per_piece = width // QB
    for f, out in zip(chunks, outs):
        start = pl.multiple_of(place_ref[f] * width, width)

        def one_expert(e, carry):
            block = down_ref[e, :, pl.ds(start, width)]
            base = e * (hidden // QB) * (features // QB) + place_ref[f] * per_piece
            right = jnp.concatenate(
                [
                    scaled(
                        block[:, n * QB : (n + 1) * QB],
                        [down_fac[base + i * (features // QB) + n] for i in range(hidden // QB)],
                    )
                    for n in range(per_piece)
                ],
                axis=1,
            )
            value = jnp.dot(act_ref[e], right, preferred_element_type=jnp.float32).astype(jnp.bfloat16)
            for p in range(n_pair):
                partial[p, pl.ds(pl.multiple_of(e * slot, slot), slot), :] = value[p * slot : (p + 1) * slot]
            return carry

        lax.fori_loop(0, experts, one_expert, 0)
        for p in range(n_pair):
            out[pl.ds(p * pair, pair), :] = jnp.dot(
                comb_ref[p], partial[p], preferred_element_type=jnp.float32
            ).astype(jnp.bfloat16)


def on_device(n_expert, n_head, residual_in, norm_gain, expert_ids, route_scores,
              gate_weight, up_weight, down_weight, gate_exp, up_exp, down_exp):
    tokens, width = residual_in.shape
    experts, features, hidden = gate_weight.shape
    split = n_expert * n_head <= 16
    vmem, smem = pl.BlockSpec(memory_space=pltpu.VMEM), pl.BlockSpec(memory_space=pltpu.SMEM)
    packed = pl.pallas_call(
        pack_kernel,
        out_shape=jax.ShapeDtypeStruct((tokens + EXTRA, width), jnp.bfloat16),
        in_specs=[vmem] * 4,
        out_specs=vmem,
        compiler_params=pltpu.CompilerParams(vmem_limit_bytes=2 * MIB),
        name="pack",
    )(residual_in, norm_gain[None, :], expert_ids.T, route_scores.T)
    head, expert = lax.axis_index("head"), lax.axis_index("expert")

    def swap(value, bit):
        return lax.ppermute(value, "head", [(i, i ^ bit) for i in range(n_head)])

    def shift(value, k):
        return lax.ppermute(value, "expert", [(i, (i + k) % n_expert) for i in range(n_expert)])

    bits = [1 << i for i in range(n_head.bit_length() - 1)]
    if split:
        pieces = {0: [packed] + [shift(packed, k) for k in range(1, n_expert)]}
        for bit in reversed(bits):
            for f in list(pieces):
                pieces[f | bit] = [swap(value, bit) for value in pieces[f]]
        gathered = [value for f in range(n_head) for value in pieces[f]]
        heads = [head ^ f for f in range(n_head)]
    else:
        gathered = [lax.all_gather(lax.all_gather(packed, "expert"), "head")]
        heads = [jnp.int32(f) for f in range(n_head)]
    place = jnp.stack(heads + [expert * experts]).astype(jnp.int32)
    factors = [power_two(x).reshape(-1) for x in (gate_exp, up_exp, down_exp)]
    n_pair, pair, slot = n_expert // 2, 2 * tokens, 2 * CAP
    act, comb = pl.pallas_call(
        functools.partial(up_kernel, n_head, n_expert, split),
        out_shape=(
            jax.ShapeDtypeStruct((experts, n_pair * slot, hidden), jnp.bfloat16),
            jax.ShapeDtypeStruct((n_pair, pair, experts * slot), jnp.bfloat16),
        ),
        in_specs=[smem] * 3 + [vmem] * (len(gathered) + 2),
        out_specs=(vmem, vmem),
        scratch_shapes=[
            pltpu.VMEM((n_expert * tokens, features), jnp.bfloat16),
            pltpu.VMEM((experts * slot, pair), jnp.bfloat16),
            pltpu.VMEM((experts, n_pair * slot, features), jnp.bfloat16),
        ],
        compiler_params=pltpu.CompilerParams(vmem_limit_bytes=UP_VMEM * MIB),
        name="up",
    )(place, factors[0], factors[1], *gathered, VM(gate_weight), VM(up_weight))

    def down(chunks):
        return pl.pallas_call(
            functools.partial(down_kernel, chunks, n_head),
            out_shape=[jax.ShapeDtypeStruct((n_expert * tokens, width), jnp.bfloat16)] * len(chunks),
            in_specs=[smem] * 2 + [vmem] * 3,
            out_specs=[vmem] * len(chunks),
            scratch_shapes=[pltpu.VMEM((n_pair, experts * slot, width), jnp.bfloat16)],
            compiler_params=pltpu.CompilerParams(vmem_limit_bytes=DOWN_VMEM * MIB),
            name="down" + "".join(str(c) for c in chunks),
        )(place, factors[2], act, comb, VM(down_weight))

    def add(a, b):
        return (a.astype(jnp.float32) + b.astype(jnp.float32)).astype(jnp.bfloat16)

    own = residual_in.astype(jnp.float32)
    if split:
        order = list(range(n_head))[::-1]
        sums = dict(zip(order, down(order)))
        for bit in bits:
            for f in [f for f in list(sums) if f & bit]:
                sums[f ^ bit] = add(sums[f ^ bit], swap(sums.pop(f), bit))
        mine = sums[0].reshape(n_expert, tokens, width)
        combined = mine[0].astype(jnp.float32)
        for k in range(1, n_expert):
            combined = combined + shift(mine[n_expert - k], k).astype(jnp.float32)
    else:
        parts = jnp.stack(down(list(range(n_head))))
        mine = lax.psum_scatter(parts, "head", scatter_dimension=0)
        mine = mine.reshape(n_expert, tokens, width)
        combined = lax.psum_scatter(mine, "expert", scatter_dimension=0).astype(jnp.float32)
    return (own + combined).astype(jnp.bfloat16)


UP_VMEM = 24
DOWN_VMEM = 16


def VM(x):
    return pltpu.with_memory_space_constraint(x, pltpu.VMEM)


def solution(mesh):
    placed = (
        P(("group", "expert"), "head"),
        P("head"),
        P(("group", "expert"), None),
        P(("group", "expert"), None),
        P("expert", None, "head"),
        P("expert", None, "head"),
        P("expert", "head", None),
        P("expert", None, "head"),
        P("expert", None, "head"),
        P("expert", "head", None),
    )
    return jax.shard_map(
        functools.partial(on_device, mesh.shape["expert"], mesh.shape["head"]),
        mesh=mesh,
        in_specs=placed,
        out_specs=P(("group", "expert"), "head"),
        check_vma=False,
    )
```

```python
import functools

import jax
import jax.numpy as jnp
from jax import lax
from jax.experimental import pallas as pl
from jax.experimental.pallas import tpu as pltpu
from jax.sharding import PartitionSpec as P

QB = 128
CAP = 24
EXTRA = 16
EPSILON = 1e-06
MIB = 1 << 20
UP_VMEM = 10
DOWN_VMEM = 4
UNROLL = 4
GROUP = 4


def power_two(exponent):
    magnitude = jnp.left_shift(jnp.ones_like(exponent), jnp.abs(exponent)).astype(jnp.float32)
    return jnp.where(exponent >= 0, magnitude, 1.0 / magnitude)


def pack_kernel(rows_hbm, gain_hbm, ids_hbm, scores_hbm, *refs):
    out_ref, ids_ref, scores_ref, gain_ref, sems = refs[-5:]
    tokens, width = rows_hbm.shape
    top = ids_ref.shape[0]
    moves = [
        pltpu.make_async_copy(ids_hbm, ids_ref, sems.at[0]),
        pltpu.make_async_copy(scores_hbm, scores_ref, sems.at[1]),
        pltpu.make_async_copy(rows_hbm, out_ref.at[pl.ds(0, tokens), :], sems.at[2]),
        pltpu.make_async_copy(gain_hbm, gain_ref, sems.at[3]),
    ]
    for move in moves:
        move.start()
    moves[3].wait()
    gain = jnp.broadcast_to(gain_ref[...].astype(jnp.float32)[None, :], (EXTRA - top, width))
    moves[0].wait()
    moves[1].wait()
    raised = jnp.exp(scores_ref[...])
    weights = raised / jnp.sum(raised, axis=0, keepdims=True)
    routes = jnp.concatenate((ids_ref[...].astype(jnp.float32), weights), axis=1)
    if width > 2 * tokens:
        routes = jnp.concatenate((routes, jnp.zeros((top, width - 2 * tokens), jnp.float32)), axis=1)
    out_ref[tokens:, :] = jnp.concatenate((routes, gain), axis=0).astype(jnp.bfloat16)
    moves[2].wait()


def scaled(block, exponents):
    parts = []
    for i, value in enumerate(exponents):
        piece = block[i * QB : (i + 1) * QB]
        by = jnp.left_shift(1, value + 15).astype(jnp.float32) * (1.0 / 32768.0)
        by = jnp.full((16, QB), by, jnp.float32).astype(jnp.bfloat16)
        parts.append((piece.reshape(QB // 16, 16, QB) * by[None]).reshape(QB, QB))
    return parts[0] if len(parts) == 1 else jnp.concatenate(parts, axis=0)


def head_of(f, split):
    return lax.axis_index("head") ^ f if split else f


def up_kernel(n_head, n_block, split, group, gate_exp, up_exp, *refs):
    n_piece = n_head * n_block if split else 1
    pieces = refs[:n_piece]
    gate_ref, up_ref, act_ref, comb_ref, normed, taken, slots = refs[n_piece:]

    def piece(f, j):
        return pieces[f * n_block + j] if split else pieces[0].at[f, j]

    experts, features, hidden = gate_ref.shape
    width = features // n_head
    tokens = normed.shape[0] // n_block
    pair = 2 * tokens
    slot = 2 * CAP
    cols = hidden // QB
    top = 8
    n_pair = n_block // 2
    for j in range(n_block):
        total = jnp.zeros((tokens, 1), jnp.float32)
        for f in range(n_head):
            value = piece(f, j)[:tokens, :].astype(jnp.float32)
            total = total + jnp.sum(value * value, axis=1, keepdims=True)
        scale = lax.rsqrt(total / features + EPSILON)
        for f in range(n_head):
            value = piece(f, j)[:tokens, :].astype(jnp.float32)
            gain = piece(f, j)[tokens + top : tokens + top + 8, :].astype(jnp.float32)[0:1, :]
            normed[pl.ds(j * tokens, tokens), pl.ds(f * width, width)] = (
                value * scale * gain
            ).astype(jnp.bfloat16)
    first = lax.axis_index("expert") * experts
    row = lax.broadcasted_iota(jnp.int32, (pair, pair), 0)
    col = lax.broadcasted_iota(jnp.int32, (pair, pair), 1)
    before = ((row < col) & ((row >= tokens) | (col < tokens))).astype(jnp.bfloat16)
    expert = (lax.broadcasted_iota(jnp.int32, (experts, pair), 0) + first).astype(jnp.float32)
    second = lax.broadcasted_iota(jnp.int32, (experts, pair), 1) >= tokens
    slot_no = lax.broadcasted_iota(jnp.int32, (slot, pair), 0).astype(jnp.float32)
    for p in range(n_block // 2):
        lists = [piece(0, 2 * p + i)[tokens : tokens + top, : 2 * tokens].astype(jnp.float32) for i in range(2)]
        ids = jnp.concatenate([x[:, :tokens] for x in lists], axis=1)
        weights = jnp.concatenate([x[:, tokens:] for x in lists], axis=1)
        named = jnp.zeros((experts, pair), jnp.float32)
        weight = jnp.zeros((experts, pair), jnp.float32)
        for k in range(top):
            same = ids[k : k + 1, :] == expert
            named = jnp.where(same, 1.0, named)
            weight = jnp.where(same, weights[k : k + 1, :], weight)
        rank = jnp.dot(named.astype(jnp.bfloat16), before, preferred_element_type=jnp.float32)
        target = jnp.where(named > 0, rank + jnp.where(second, float(CAP), 0.0), -1.0)
        back = []
        for e in range(experts):
            here = target[e : e + 1, :] == slot_no
            taken[p, pl.ds(e * slot, slot), :] = jnp.where(here, 1.0, 0.0).astype(jnp.bfloat16)
            back.append(jnp.where(here, weight[e : e + 1, :], 0.0))
        comb_ref[p] = jnp.transpose(jnp.concatenate(back, axis=0)).astype(jnp.bfloat16)

    per_piece = width // QB
    step = min(features, 512)

    def one_group(g, carry):
        for p in range(n_pair):
            chosen = taken[p, pl.ds(pl.multiple_of(g * (group * slot), group * slot), group * slot), :]
            for n in range(features // step):
                rows = jnp.dot(
                    chosen,
                    normed[pl.ds(p * pair, pair), pl.ds(n * step, step)],
                    preferred_element_type=jnp.float32,
                ).astype(jnp.bfloat16)
                slots[:, pl.ds(p * slot, slot), pl.ds(n * step, step)] = rows.reshape(group, slot, step)
        for i in range(group):
            e = g * group + i
            outs = []
            for ref, exp in ((gate_ref, gate_exp), (up_ref, up_exp)):
                acc = None
                for f in range(n_head):
                    at = head_of(f, split)
                    start = pl.multiple_of(at * width, width)
                    left = slots[i, :, pl.ds(f * width, width)]
                    block = ref[e, pl.ds(start, width), :]
                    right = [
                        scaled(
                            block[:, n * QB : (n + 1) * QB],
                            [exp[e, n, at * per_piece + k] for k in range(per_piece)],
                        )
                        for n in range(cols)
                    ]
                    right = right[0] if cols == 1 else jnp.concatenate(right, axis=1)
                    term = jnp.dot(left, right, preferred_element_type=jnp.float32)
                    acc = term if acc is None else acc + term
                outs.append(acc)
            gate_out, up_out = outs
            act = gate_out / (1.0 + jnp.exp(-gate_out)) * up_out
            act_ref[e] = act.astype(jnp.bfloat16)
        return carry

    lax.fori_loop(0, experts // group, one_group, 0)


def down_kernel(f, n_head, split, down_exp, act_ref, comb_ref, down_ref, *refs):
    outs, partial = refs[:-1], refs[-1]
    experts, hidden, features = down_ref.shape
    width = features // n_head
    n_pair, pair, _ = comb_ref.shape
    slot = 2 * CAP
    per_piece = width // QB
    at = head_of(f, split)
    start = pl.multiple_of(at * width, width)

    def one_expert(e, carry):
        block = down_ref[e, :, pl.ds(start, width)]
        right = jnp.concatenate(
            [
                scaled(
                    block[:, n * QB : (n + 1) * QB],
                    [down_exp[e, i, at * per_piece + n] for i in range(hidden // QB)],
                )
                for n in range(per_piece)
            ],
            axis=1,
        )
        value = jnp.dot(act_ref[e], right, preferred_element_type=jnp.float32).astype(jnp.bfloat16)
        for p in range(n_pair):
            partial[p, pl.ds(pl.multiple_of(e * slot, slot), slot), :] = value[p * slot : (p + 1) * slot]
        return carry

    lax.fori_loop(0, experts, one_expert, 0, unroll=min(experts, UNROLL))
    for p in range(n_pair):
        value = jnp.dot(comb_ref[p], partial[p], preferred_element_type=jnp.float32).astype(jnp.bfloat16)
        if len(outs) == 1:
            outs[0][pl.ds(p * pair, pair), :] = value
        else:
            outs[2 * p][...] = value[: pair // 2]
            outs[2 * p + 1][...] = value[pair // 2 :]


def on_device(n_expert, n_head, residual_in, norm_gain, expert_ids, route_scores,
              gate_weight, up_weight, down_weight, gate_exp, up_exp, down_exp):
    tokens, width = residual_in.shape
    experts, features, hidden = gate_weight.shape
    split = n_head == 4 and n_expert <= 4
    vmem, smem = pl.BlockSpec(memory_space=pltpu.VMEM), pl.BlockSpec(memory_space=pltpu.SMEM)
    hbm = pl.BlockSpec(memory_space=pltpu.HBM)
    top = expert_ids.shape[1]
    packed = pl.pallas_call(
        pack_kernel,
        out_shape=jax.ShapeDtypeStruct((tokens + EXTRA, width), jnp.bfloat16),
        in_specs=[hbm] * 7,
        out_specs=vmem,
        scratch_shapes=[
            pltpu.VMEM((top, tokens), jnp.int32),
            pltpu.VMEM((top, tokens), jnp.float32),
            pltpu.VMEM((width,), jnp.bfloat16),
            pltpu.SemaphoreType.DMA((4,)),
        ],
        compiler_params=pltpu.CompilerParams(vmem_limit_bytes=MIB),
        name="pack",
    )(HB(residual_in), HB(norm_gain), HB(expert_ids.T), HB(route_scores.T), HB(gate_weight), HB(up_weight), HB(down_weight))

    def swap(value, bit):
        return lax.ppermute(value, "head", [(i, i ^ bit) for i in range(n_head)])

    def shift(value, k):
        return lax.ppermute(value, "expert", [(i, (i + k) % n_expert) for i in range(n_expert)])

    bits = [1 << i for i in range(n_head.bit_length() - 1)]
    if split:
        pieces = {0: [packed] + [shift(packed, k) for k in range(1, n_expert)]}
        for bit in reversed(bits):
            for f in list(pieces):
                pieces[f | bit] = [swap(value, bit) for value in pieces[f]]
        gathered = [value for f in range(n_head) for value in pieces[f]]
    else:
        gathered = [lax.all_gather(lax.all_gather(packed, "expert"), "head")]
    group = min(experts, GROUP)
    gate_exp, up_exp = (jnp.transpose(x, (0, 2, 1)) for x in (gate_exp, up_exp))
    n_pair, pair, slot = n_expert // 2, 2 * tokens, 2 * CAP
    act, comb = pl.pallas_call(
        functools.partial(up_kernel, n_head, n_expert, split, group),
        out_shape=(
            jax.ShapeDtypeStruct((experts, n_pair * slot, hidden), jnp.bfloat16),
            jax.ShapeDtypeStruct((n_pair, pair, experts * slot), jnp.bfloat16),
        ),
        in_specs=[smem] * 2 + [vmem] * (len(gathered) + 2),
        out_specs=(vmem, vmem),
        scratch_shapes=[
            pltpu.VMEM((n_expert * tokens, features), jnp.bfloat16),
            pltpu.VMEM((n_pair, experts * slot, pair), jnp.bfloat16),
            pltpu.VMEM((group, n_pair * slot, features), jnp.bfloat16),
        ],
        compiler_params=pltpu.CompilerParams(vmem_limit_bytes=UP_VMEM * MIB),
        name="up",
    )(gate_exp, up_exp, *gathered, VM(gate_weight), VM(up_weight))

    def down(f, blocks):
        rows = n_expert * tokens // blocks
        return pl.pallas_call(
            functools.partial(down_kernel, f, n_head, split),
            out_shape=[jax.ShapeDtypeStruct((rows, width), jnp.bfloat16)] * blocks,
            in_specs=[smem] + [vmem] * 3,
            out_specs=[vmem] * blocks,
            scratch_shapes=[pltpu.VMEM((n_pair, experts * slot, width), jnp.bfloat16)],
            compiler_params=pltpu.CompilerParams(vmem_limit_bytes=DOWN_VMEM * MIB),
            name="down" + str(f),
        )(down_exp, act, comb, VM(down_weight))

    def add(*terms):
        return functools.reduce(jnp.add, [t.astype(jnp.float32) for t in terms]).astype(jnp.bfloat16)

    def rows_of(value, j):
        return value[j * tokens : (j + 1) * tokens]

    own = residual_in.astype(jnp.float32)
    if split:
        (far,) = down(3, 1)
        near = down(2, n_expert)
        far = swap(far, 1)
        order = list(range(1, n_expert)) + [0]
        crossed = {j: swap(add(near[j], rows_of(far, j)), 2) for j in order}
        (beside,) = down(1, 1)
        mine = down(0, n_expert)
        beside = swap(beside, 1)
        combined = own
        for j in order:
            total = add(mine[j], rows_of(beside, j), crossed[j])
            combined = combined + (shift(total, n_expert - j) if j else total).astype(jnp.float32)
    else:
        parts = jnp.stack([down(f, 1)[0] for f in range(n_head)])
        mine = lax.psum_scatter(parts, "head", scatter_dimension=0)
        mine = mine.reshape(n_expert, tokens, width)
        combined = own + lax.psum_scatter(mine, "expert", scatter_dimension=0).astype(jnp.float32)
    return combined.astype(jnp.bfloat16)


def HB(x):
    return pltpu.with_memory_space_constraint(x, pltpu.HBM)


def VM(x):
    return pltpu.with_memory_space_constraint(x, pltpu.VMEM)


def solution(mesh):
    placed = (
        P(("group", "expert"), "head"),
        P("head"),
        P(("group", "expert"), None),
        P(("group", "expert"), None),
        P("expert", None, "head"),
        P("expert", None, "head"),
        P("expert", "head", None),
        P("expert", None, "head"),
        P("expert", None, "head"),
        P("expert", "head", None),
    )
    return jax.shard_map(
        functools.partial(on_device, mesh.shape["expert"], mesh.shape["head"]),
        mesh=mesh,
        in_specs=placed,
        out_specs=P(("group", "expert"), "head"),
        check_vma=False,
    )
```
